32 devices in a mesh: group: 2 (over y), row: 8 (over z, x), col: 2 (over core).
Axes of the slice: x: 2, y: 2, z: 4, core: 2. Of those that a mesh axis runs over, the one named last changes fastest.
Arguments:
- map_in: bfloat16 [192, 96, 48], P(('group', 'row'), 'col'), parts along dimension 0, may hold values from -6 to 6
- embedding: bfloat16 [192, 96], P(('group', 'row')), parts along dimension 0, may hold values from -6 to 6
- w_row: bfloat16 [96, 48], replicated, may hold values from -0.625 to 0.625
- w_col: bfloat16 [96, 48], replicated, may hold values from -0.625 to 0.625
- first_kernel_weight: bfloat16 [3, 3, 48, 48], replicated, may hold values from -0.3125 to 0.3125
- first_bias: float32 [48], replicated, may hold values from -0.5 to 0.5
- second_kernel_weight: bfloat16 [3, 3, 48, 48], replicated, may hold values from -0.3125 to 0.3125
- second_bias: float32 [48], replicated, may hold values from -0.5 to 0.5
- w_mix: bfloat16 [48, 48], replicated, may hold values from -0.875 to 0.875
- b_mix: float32 [48], replicated, may hold values from -0.5 to 0.5
- w_head: float32 [48], replicated, may hold values from -0.875 to 0.875
Outputs:
- contacts: float32 [192, 96], P(('group', 'row'), 'col'), parts along dimension 0
The draws below stay inside these ranges and needn't reach their ends.
There are 2 independent parts, one for each index of `group`. The reference program is written for one: setup_inputs(seed, part) draws one part's arguments, and reference() takes and returns one part's arrays. A program takes and returns all parts, laid end to end along the dimension named above; an argument that names none is the same for every part. Nothing has to cross between parts.
All inputs are finite; a program needn't handle non-finite values.
Results may differ from the reference program's by a relative error of at most 0.0055.
Values may be sent and summed in bfloat16 or wider, within the bound.
A program may use at most 64 MiB of HBM per device.

```python
import jax
import jax.numpy as jnp
from jax import lax

CH = 48
E = 96
FIRST_DILATION = 4
SECOND_DILATION = 8
ROWS_DEV = 12
BINS = 96


def level_of(key, extent, shards, smallest, top_value):
    def one(dim, parts):
        steps = jax.random.uniform(jax.random.fold_in(jax.random.fold_in(key, 6), dim), (parts,), jnp.float32, smallest / len(shards), top_value / len(shards))
        return jnp.repeat(jnp.exp(steps), extent[dim] // parts).reshape((-1,) + (1,) * (len(extent) - dim - 1))

    level = one(*shards[0])
    for cut in shards[1:]:
        level = level * one(*cut)
    return level


def noise(stream_key, shape, deviation, most, shards=(), held_as=jnp.bfloat16):
    entries = jax.random.normal(stream_key, shape, jnp.float32) * deviation
    if len(shards) > 0:
        entries = level_of(stream_key, shape, shards, -0.22, 0.18) * entries
    return jnp.clip(entries, min=-most, max=most).astype(held_as)


def setup_inputs(seed: int = 0, part: int = 0) -> dict:
    splits = jax.random.split(jax.random.key(seed), 12)
    part_keys = jax.random.split(jax.random.fold_in(splits[11], part), 12)
    map_in = noise(part_keys[0], (BINS, BINS, CH), 1.0, 6.0, ((0, 8), (1, 2)))
    embedding = noise(part_keys[1], (BINS, E), 1.0, 6.0, ((0, 8),))
    w_row = noise(splits[2], (E, CH), E ** -0.5, 0.625)
    w_col = noise(splits[3], (E, CH), E ** -0.5, 0.625)
    first_kernel_weight = noise(splits[4], (3, 3, CH, CH), (9 * CH) ** -0.5, 0.3125)
    first_bias = jnp.clip(jax.random.uniform(splits[5], (CH,), jnp.float32, -0.5, 0.5), -0.5, 0.5)
    second_kernel_weight = noise(splits[6], (3, 3, CH, CH), (9 * CH) ** -0.5, 0.3125)
    second_bias = jnp.clip(jax.random.uniform(splits[7], (CH,), jnp.float32, -0.5, 0.5), -0.5, 0.5)
    w_mix = noise(splits[8], (CH, CH), CH ** -0.5, 0.875)
    b_mix = jnp.clip(jax.random.uniform(splits[9], (CH,), jnp.float32, -0.5, 0.5), -0.5, 0.5)
    w_head = noise(splits[10], (CH,), CH ** -0.5, 0.875, (), jnp.float32)
    return {"map_in": map_in, "embedding": embedding, "w_row": w_row, "w_col": w_col, "first_kernel_weight": first_kernel_weight, "first_bias": first_bias, "second_kernel_weight": second_kernel_weight, "second_bias": second_bias, "w_mix": w_mix, "b_mix": b_mix, "w_head": w_head}


def residual_block(field, weight, bias, spacing):
    bins_total = field.shape[0]
    block = ROWS_DEV
    padded = jnp.pad(field, ((spacing, spacing), (spacing, spacing), (0, 0)))
    kernel = weight.astype(jnp.float32)

    def one_block(start):
        piece = lax.dynamic_slice_in_dim(padded, start, block + 2 * spacing, 0)
        active = jnp.maximum(piece, 0).astype(jnp.float32)
        convolved = lax.conv_general_dilated(
            active[None], kernel, (1, 1), "VALID", rhs_dilation=(spacing, spacing),
            dimension_numbers=("NHWC", "HWIO", "NHWC"), precision=lax.Precision.HIGHEST)[0]
        own_rows = lax.dynamic_slice_in_dim(field, start, block, 0).astype(jnp.float32)
        return (own_rows + convolved + bias).astype(jnp.bfloat16)

    starts = jnp.arange(bins_total // block, dtype=jnp.int32) * block
    return lax.map(one_block, starts).reshape(field.shape)


def reference(map_in, embedding, w_row, w_col, first_kernel_weight, first_bias, second_kernel_weight, second_bias, w_mix, b_mix, w_head):
    row_terms = jnp.dot(embedding, w_row, preferred_element_type=jnp.float32)
    col_terms = jnp.dot(embedding, w_col, preferred_element_type=jnp.float32)
    contact_grid = (map_in.astype(jnp.float32) + row_terms[:, None, :] + col_terms[None, :, :]).astype(jnp.bfloat16)
    first_layer = residual_block(contact_grid, first_kernel_weight, first_bias, FIRST_DILATION)
    second_layer = residual_block(first_layer, second_kernel_weight, second_bias, SECOND_DILATION)
    block = ROWS_DEV
    mixing = w_mix.astype(jnp.float32)

    def head_block(start):
        own_rows = lax.dynamic_slice_in_dim(second_layer, start, block, 0).astype(jnp.float32)
        mirror = jnp.swapaxes(lax.dynamic_slice_in_dim(second_layer, start, block, 1), 0, 1).astype(jnp.float32)
        symmetric = ((own_rows + mirror) * 0.5).astype(jnp.bfloat16)
        mixture = jnp.einsum("rch,hk->rck", symmetric.astype(jnp.float32), mixing,
                             precision=lax.Precision.HIGHEST) + b_mix
        mixture = jnp.maximum(mixture, 0.0)
        return jnp.sum(mixture * w_head, axis=-1)

    starts = jnp.arange(map_in.shape[0] // block, dtype=jnp.int32) * block
    return lax.map(head_block, starts).reshape(map_in.shape[0], map_in.shape[1])
```

```python
import functools

import jax
import jax.numpy as jnp
from jax import lax
from jax.experimental import pallas as pl
from jax.experimental.pallas import tpu as pltpu
from jax.sharding import PartitionSpec as P

FIRST_DILATION = 4
SECOND_DILATION = 8


def padded(array, sides, width):
    for axis, dim in sides:
        peers, length = (lax.axis_size(axis), array.shape[dim])
        up = [(i, (i + 1) % peers) for i in range(peers - 1)]
        down = [(j, i) for i, j in up]
        last = lax.slice_in_dim(array, length - width, length, axis=dim)
        leading = lax.slice_in_dim(array, 0, width, axis=dim)
        before = lax.ppermute(last, axis, up)
        after = lax.ppermute(leading, axis, down)
        array = jnp.concatenate([before, array, after], axis=dim)
    return array


def swapped(value, axis, bit):
    mask = 2**bit
    pairs = [(source, source ^ mask) for source in range(lax.axis_size(axis))]
    return lax.ppermute(value, axis, pairs)


def dilated_conv(active, weight, spacing, out_rows, out_cols):
    windows = []
    for tap_row in range(3):
        for tap_col in range(3):
            windows.append(
                active[
                    tap_row * spacing : tap_row * spacing + out_rows,
                    tap_col * spacing : tap_col * spacing + out_cols,
                ]
            )
    stacked = jnp.concatenate(windows, axis=-1)
    flat_weight = weight.reshape(9 * weight.shape[2], weight.shape[3])
    return jnp.einsum("rch,hk->rck", stacked, flat_weight, preferred_element_type=jnp.float32)


LANES = 128
HALF = 64
SIDE = 16
FUSED_VMEM = 8 * 2**20


def one_hot(rows, columns, offsets):
    r = lax.broadcasted_iota(jnp.int32, (rows, columns), 0)
    c = lax.broadcasted_iota(jnp.int32, (rows, columns), 1)
    hit = c == r + offsets[0]
    for offset in offsets[1:]:
        hit = hit | (c == r + offset)
    return jnp.where(hit, 1.0, 0.0)


def mm(a, b, precision=None):
    return jnp.dot(a, b, preferred_element_type=jnp.float32, precision=precision)


def fused_kernel(
    n,
    m_ref,
    e_ref,
    wr_ref,
    wc_ref,
    w1_ref,
    b1_ref,
    w2_ref,
    b2_ref,
    wm_ref,
    bm_ref,
    wh_ref,
    out_ref,
    pk,
    eb,
    ct,
    rt,
    xb,
    rb,
    pc,
    l1,
    rb2,
    pc2,
    wa,
    wb,
    yb,
    sb,
    gb,
    tb,
    send,
    recv,
    esend,
    erecv,
    msend,
    mrecv,
    lsem,
):
    bf, f32 = jnp.bfloat16, jnp.float32
    rows, cols, ch = m_ref.shape
    hr = rows // 2
    width = cols + SIDE
    per = cols // rows
    R = lax.axis_index("row")
    C = lax.axis_index("col")
    O = 1 - C
    group = lax.axis_index("group")
    mesh_type = pl.DeviceIdType.MESH

    barrier = pltpu.get_barrier_semaphore()
    for k in range(n):
        for col in (C, O):
            if k == 0 and col is C:
                continue
            pl.semaphore_signal(
                barrier, inc=1, device_id=(group, lax.rem(R + k, n), col), device_id_type=mesh_type
            )

    low = one_hot(ch, LANES, (0,)).astype(bf)
    high = one_hot(ch, LANES, (HALF,)).astype(bf)
    both = one_hot(ch, LANES, (0, HALF)).astype(bf)
    own_at = pl.multiple_of(SIDE * C, SIDE)
    tile = m_ref[...]
    packed = mm(tile[:hr].reshape(hr * cols, ch), low) + mm(tile[hr:].reshape(hr * cols, ch), high)
    pk[1, :, pl.ds(own_at, cols), :] = packed.astype(bf).reshape(hr, cols, LANES)
    eb[R] = e_ref[...]

    pl.semaphore_wait(barrier, 2 * n - 1)

    def remote(src, dst, s, r, row, col):
        return pltpu.make_async_remote_copy(
            src_ref=src,
            dst_ref=dst,
            send_sem=s,
            recv_sem=r,
            device_id=(group, row, col),
            device_id_type=mesh_type,
        )

    embs = []
    for k in range(1, n):
        copy = remote(
            eb.at[R], eb.at[R], esend.at[k - 1], erecv.at[k - 1], lax.rem(R + k, n), C
        )
        copy.start()
        embs.append(copy)

    own_src = pk.at[1, :, pl.ds(own_at, cols), :]
    side_src = pk.at[1, :, pl.ds(pl.multiple_of(cols - SIDE - (cols - 2 * SIDE) * C, SIDE), SIDE), :]
    side_at = pl.ds(pl.multiple_of(cols * C, SIDE), SIDE)
    above = jnp.maximum(R - 1, 0)
    below = jnp.minimum(R + 1, n - 1)
    to_below = remote(
        own_src, pk.at[0, :, pl.ds(own_at, cols), :], send.at[0], recv.at[0], below, C
    )
    to_above = remote(
        own_src, pk.at[2, :, pl.ds(own_at, cols), :], send.at[1], recv.at[1], above, C
    )
    to_side = remote(side_src, pk.at[1, :, side_at, :], send.at[2], recv.at[2], R, O)
    side_below = remote(side_src, pk.at[0, :, side_at, :], send.at[3], recv.at[3], below, O)
    side_above = remote(side_src, pk.at[2, :, side_at, :], send.at[4], recv.at[4], above, O)

    @pl.when(R < n - 1)
    def _():
        to_below.start()
        side_below.start()

    @pl.when(R > 0)
    def _():
        to_above.start()
        side_above.start()

    to_side.start()

    def pack_weight(w_ref, dst):
        dst[...] = jnp.zeros_like(dst)
        taps = ((0, 0), (0, 2), (1, 0), (1, 2), (2, 0), (2, 2), (0, 1), (2, 1), (1, 1))
        for at, (a, b) in enumerate(taps):
            dst[at * HALF : at * HALF + ch, :] = mm(w_ref[a, b], both).astype(bf)

    pack_weight(w1_ref, wa)
    pack_weight(w2_ref, wb)
    exact = lax.Precision.HIGHEST
    bias1 = mm(b1_ref[...], both.astype(f32), exact)
    bias2 = mm(b2_ref[...], both.astype(f32), exact)
    wr = mm(wr_ref[...], both).astype(bf)
    wc = mm(wc_ref[...], both).astype(bf)
    eye = one_hot(ch, ch, (0,))
    mix_rows = jnp.concatenate([wm_ref[...], jnp.zeros((LANES - ch, ch), bf)], axis=0)
    nt = (((1,), (1,)), ((), ()))
    mix_t = lax.dot_general(eye.astype(bf), mix_rows, nt, preferred_element_type=f32).astype(bf)
    bm = jnp.sum(jnp.where(eye > 0, bm_ref[...], 0.0), axis=1, keepdims=True)
    wh = jnp.sum(jnp.where(eye > 0, wh_ref[...], 0.0), axis=1, keepdims=True)

    for copy in embs:
        copy.wait()
    for k in range(n):
        block = eb[k]
        ct[k * rows : (k + 1) * rows, :] = mm(block, wc)
        rt[k] = mm(block, wr)
    col_terms = ct[pl.ds(pl.multiple_of((n * rows - width) * C, 8), width), :]

    to_side.wait()

    @pl.when(R > 0)
    def _():
        to_below.wait_recv()
        side_below.wait_recv()

    @pl.when(R < n - 1)
    def _():
        to_above.wait_recv()
        side_above.wait_recv()

    lane = lax.broadcasted_iota(jnp.int32, (1, LANES), 1)
    lower = lane < HALF
    col_id = lax.broadcasted_iota(jnp.int32, (width, 1), 0)

    def column_pair(v, d):
        before = jnp.where(col_id < d, 0.0, pltpu.roll(v, d, axis=0))
        after = jnp.where(col_id >= width - d, 0.0, pltpu.roll(v, width - d, axis=0))
        return jnp.where(lower, before, after)

    for b in range(3):
        at = jnp.clip(R + b - 1, 0, n - 1)
        terms = rt[at]
        valid = (R > 0) if b == 0 else (R < n - 1) if b == 2 else None
        for i in range(hr):
            v = pk[b, i].astype(f32)
            turned = pltpu.roll(v, HALF, axis=1)
            for half, x in ((0, jnp.where(lower, v, turned)), (1, jnp.where(lower, turned, v))):
                r = i + half * hr
                x = (x + terms[r : r + 1, :] + col_terms).astype(bf)
                x = x.astype(f32)
                if valid is not None:
                    x = jnp.where(valid, x, 0.0)
                row = b * rows + r
                xb[row] = x.astype(bf)
                x = jnp.maximum(x, 0.0)
                rb[row] = x.astype(bf)
                pc[row] = column_pair(x, FIRST_DILATION).astype(bf)

    def conv(p, r, w, first, count, d, at, size):
        window = pl.ds(at, size)

        def take(ref, shift):
            return ref[first + shift : first + shift + count, window, :].reshape(
                count * size, LANES
            )

        outer = jnp.where(lower, take(r, 0).astype(f32), take(r, 2 * d).astype(f32)).astype(bf)
        left = jnp.concatenate(
            [take(p, 0), take(p, d), take(p, 2 * d), outer, take(r, d)], axis=1
        )
        return mm(left, w[...]).reshape(count, size, LANES)

    d2 = SECOND_DILATION
    ext = rows + 2 * d2
    step = 7 if ext % 7 == 0 else 1
    for t in range(0, ext, step):
        acc = conv(pc, rb, wa, t, step, FIRST_DILATION, 0, width)
        for s in range(step):
            u = t + s
            x = (xb[u + FIRST_DILATION].astype(f32) + acc[s] + bias1).astype(bf).astype(f32)
            if u < d2:
                x = jnp.where(R > 0, x, 0.0)
            elif u >= d2 + rows:
                x = jnp.where(R < n - 1, x, 0.0)
            else:
                l1[u - d2] = x.astype(bf)
            x = jnp.maximum(x, 0.0)
            rb2[u] = x.astype(bf)
            pc2[u] = column_pair(x, d2).astype(bf)

    for t in range(0, rows, hr):
        acc = conv(pc2, rb2, wb, t, hr, d2, own_at, cols)
        for s in range(hr):
            base = l1[t + s, pl.ds(own_at, cols), :].astype(f32)
            yb[t + s] = (base + acc[s] + bias2).astype(bf).astype(f32)

    for i in range(hr):
        pair = jnp.where(lower, yb[i], yb[i + hr])
        for j in range(per):
            sb[j, i] = pair[j * rows : (j + 1) * rows, :].astype(bf)

    mine = lax.rem(R, per)
    quarter = lax.div(R, per)
    for j in range(per):
        peer = per * C + j
        is_self = (peer == R) & (quarter == C)
        copy = remote(sb.at[j], gb.at[mine], msend.at[j], mrecv.at[mine], peer, quarter)
        local = pltpu.make_async_copy(sb.at[j], gb.at[j], lsem)

        @pl.when(jnp.logical_not(is_self))
        def _():
            copy.start()

        @pl.when(is_self)
        def _():
            local.start()

    for j in range(per):
        peer = per * C + j
        is_self = (peer == R) & (quarter == C)
        arrival = remote(sb.at[j], gb.at[j], msend.at[j], mrecv.at[j], peer, quarter)
        local = pltpu.make_async_copy(sb.at[j], gb.at[j], lsem)

        @pl.when(jnp.logical_not(is_self))
        def _():
            arrival.wait_recv()

        @pl.when(is_self)
        def _():
            local.wait()

    pad = tb.shape[0] // cols
    for j in range(per):
        for i in range(hr):
            piece = gb[j, i].astype(f32)
            at = (j * rows + i) * pad
            tb[at : at + rows, :] = piece
            at = (j * rows + i + hr) * pad
            tb[at : at + rows, :] = pltpu.roll(piece, HALF, axis=1)

    for c in range(rows):
        mirror = tb[pl.ds(c, cols, stride=pad), :]
        symmetric = ((yb[c] + mirror) * 0.5).astype(bf)
        mixed = lax.dot_general(mix_t, symmetric, nt, preferred_element_type=f32) + bm
        out_ref[c : c + 1, :] = jnp.sum(jnp.maximum(mixed, 0.0) * wh, axis=0, keepdims=True)

    @pl.when(R < n - 1)
    def _():
        to_below.wait_send()
        side_below.wait_send()

    @pl.when(R > 0)
    def _():
        to_above.wait_send()
        side_above.wait_send()

    for j in range(per):
        peer = per * C + j
        is_self = (peer == R) & (quarter == C)
        departure = remote(sb.at[j], gb.at[j], msend.at[j], mrecv.at[j], peer, quarter)

        @pl.when(jnp.logical_not(is_self))
        def _():
            departure.wait_send()


def fused(map_in, embedding, w_row, w_col, w1, b1, w2, b2, w_mix, b_mix, w_head):
    rows, cols, ch = map_in.shape
    n = lax.axis_size("row")
    width, ext, per, hr = cols + SIDE, rows + 2 * SECOND_DILATION, cols // rows, rows // 2
    bf, f32 = jnp.bfloat16, jnp.float32
    dma = pltpu.SemaphoreType.DMA
    return pl.pallas_call(
        functools.partial(fused_kernel, n),
        out_shape=jax.ShapeDtypeStruct((rows, cols), f32),
        in_specs=[pl.BlockSpec(memory_space=pltpu.VMEM)] * 11,
        out_specs=pl.BlockSpec(memory_space=pltpu.VMEM),
        scratch_shapes=[
            pltpu.VMEM((3, hr, width, LANES), bf),
            pltpu.VMEM((n, rows, embedding.shape[1]), bf),
            pltpu.VMEM((n * rows, LANES), f32),
            pltpu.VMEM((n, rows, LANES), f32),
            pltpu.VMEM((3 * rows, width, LANES), bf),
            pltpu.VMEM((3 * rows, width, LANES), bf),
            pltpu.VMEM((3 * rows, width, LANES), bf),
            pltpu.VMEM((rows, width, LANES), bf),
            pltpu.VMEM((ext, width, LANES), bf),
            pltpu.VMEM((ext, width, LANES), bf),
            pltpu.VMEM((10 * HALF, LANES), bf),
            pltpu.VMEM((10 * HALF, LANES), bf),
            pltpu.VMEM((rows, cols, LANES), f32),
            pltpu.VMEM((per, hr, rows, LANES), bf),
            pltpu.VMEM((per, hr, rows, LANES), bf),
            pltpu.VMEM((cols * 16, LANES), f32),
            dma((5,)),
            dma((5,)),
            dma((n - 1,)),
            dma((n - 1,)),
            dma((per,)),
            dma((per,)),
            dma,
        ],
        compiler_params=pltpu.CompilerParams(collective_id=0, has_side_effects=True),
    )(
        map_in,
        embedding,
        w_row,
        w_col,
        w1,
        b1.reshape(1, ch),
        w2,
        b2.reshape(1, ch),
        w_mix,
        b_mix.reshape(1, ch),
        w_head.reshape(1, ch),
    )


def fits(rows, cols, channels, row_count, col_count):
    scratch = 2 * LANES * (cols + SIDE) * (16 * rows + 6 * SECOND_DILATION)
    halo = FIRST_DILATION + SECOND_DILATION
    return (
        scratch <= FUSED_VMEM
        and rows == halo
        and col_count == 2
        and cols % SIDE == 0
        and channels <= 48
        and cols * col_count == rows * row_count
    )


def on_device(
    map_in,
    embedding,
    w_row,
    w_col,
    first_kernel_weight,
    first_bias,
    second_kernel_weight,
    second_bias,
    w_mix,
    b_mix,
    w_head,
):
    patch_rows, patch_columns, channels = map_in.shape
    row_count = lax.axis_size("row")
    if fits(patch_rows, patch_columns, channels, row_count, lax.axis_size("col")):
        return fused(
            map_in,
            embedding,
            w_row,
            w_col,
            first_kernel_weight,
            first_bias,
            second_kernel_weight,
            second_bias,
            w_mix,
            b_mix,
            w_head,
        )
    row_at = lax.axis_index("row")
    col_at = lax.axis_index("col")
    all_bins = lax.all_gather(embedding, "row", axis=0, tiled=True)
    row_terms = jnp.dot(all_bins, w_row, preferred_element_type=jnp.float32)
    col_terms = jnp.dot(all_bins, w_col, preferred_element_type=jnp.float32)
    own_rows = lax.dynamic_slice_in_dim(row_terms, row_at * patch_rows, patch_rows, 0)
    own_cols = lax.dynamic_slice_in_dim(col_terms, col_at * patch_columns, patch_columns, 0)
    contact_grid = (
        map_in.astype(jnp.float32) + own_rows[:, None, :] + own_cols[None, :, :]
    ).astype(jnp.bfloat16)
    first_padded = padded(contact_grid, (("row", 0), ("col", 1)), FIRST_DILATION)
    first_layer = (
        contact_grid.astype(jnp.float32)
        + dilated_conv(
            jnp.maximum(first_padded, 0),
            first_kernel_weight,
            FIRST_DILATION,
            patch_rows,
            patch_columns,
        )
        + first_bias
    ).astype(jnp.bfloat16)
    second_padded = padded(first_layer, (("row", 0), ("col", 1)), SECOND_DILATION)
    second_layer = (
        first_layer.astype(jnp.float32)
        + dilated_conv(
            jnp.maximum(second_padded, 0),
            second_kernel_weight,
            SECOND_DILATION,
            patch_rows,
            patch_columns,
        )
        + second_bias
    ).astype(jnp.bfloat16)
    half_rows = patch_rows // 2
    blocks_per = row_count // 2
    arranged = second_layer.reshape(2, half_rows, blocks_per, patch_rows, channels)
    arranged = arranged.transpose(0, 2, 1, 3, 4).reshape(
        2 * blocks_per, half_rows, patch_rows, channels
    )
    exchanged = lax.all_to_all(
        lax.all_to_all(arranged, "row", split_axis=0, concat_axis=0, tiled=True),
        "col",
        split_axis=0,
        concat_axis=0,
        tiled=True,
    )
    exchanged = exchanged.reshape(2, blocks_per, half_rows, patch_rows, channels)
    top_half = row_at // blocks_per
    kept_part = lax.dynamic_index_in_dim(exchanged, top_half, 0, keepdims=False)
    sent_part = lax.dynamic_index_in_dim(exchanged, 1 - top_half, 0, keepdims=False)
    came_back = swapped(sent_part, "row", blocks_per.bit_length() - 1)
    stacked = jnp.where(
        top_half == 0, jnp.stack([kept_part, came_back]), jnp.stack([came_back, kept_part])
    )
    mirrored = stacked.transpose(3, 1, 0, 2, 4).reshape(patch_rows, patch_columns, channels)
    symmetric = ((second_layer.astype(jnp.float32) + mirrored.astype(jnp.float32)) * 0.5).astype(
        jnp.bfloat16
    )
    mixture = (
        jnp.einsum("rch,hk->rck", symmetric, w_mix, preferred_element_type=jnp.float32) + b_mix
    )
    mixture = jnp.maximum(mixture, 0.0)
    return jnp.sum(mixture * w_head, axis=-1)


def solution(mesh):
    placed = (
        P(("group", "row"), "col", None),
        P(("group", "row"), None),
        P(),
        P(),
        P(),
        P(),
        P(),
        P(),
        P(),
        P(),
        P(),
    )
    return jax.shard_map(
        on_device, mesh=mesh, in_specs=placed, out_specs=P(("group", "row"), "col"), check_vma=False
    )
```

```python
import functools

import jax
import jax.numpy as jnp
from jax import lax
from jax.experimental import pallas as pl
from jax.experimental.pallas import tpu as pltpu
from jax.sharding import PartitionSpec as P

FIRST_DILATION = 4
SECOND_DILATION = 8


def padded(array, sides, width):
    for axis, dim in sides:
        peers, length = (lax.axis_size(axis), array.shape[dim])
        up = [(i, (i + 1) % peers) for i in range(peers - 1)]
        down = [(j, i) for i, j in up]
        last = lax.slice_in_dim(array, length - width, length, axis=dim)
        leading = lax.slice_in_dim(array, 0, width, axis=dim)
        before = lax.ppermute(last, axis, up)
        after = lax.ppermute(leading, axis, down)
        array = jnp.concatenate([before, array, after], axis=dim)
    return array


def swapped(value, axis, bit):
    mask = 2**bit
    pairs = [(source, source ^ mask) for source in range(lax.axis_size(axis))]
    return lax.ppermute(value, axis, pairs)


def dilated_conv(active, weight, spacing, out_rows, out_cols):
    windows = []
    for tap_row in range(3):
        for tap_col in range(3):
            windows.append(
                active[
                    tap_row * spacing : tap_row * spacing + out_rows,
                    tap_col * spacing : tap_col * spacing + out_cols,
                ]
            )
    stacked = jnp.concatenate(windows, axis=-1)
    flat_weight = weight.reshape(9 * weight.shape[2], weight.shape[3])
    return jnp.einsum("rch,hk->rck", stacked, flat_weight, preferred_element_type=jnp.float32)


LANES = 128
HALF = 64
SIDE = 16
FUSED_VMEM = 8 * 2**20


def one_hot(rows, columns, offsets):
    r = lax.broadcasted_iota(jnp.int32, (rows, columns), 0)
    c = lax.broadcasted_iota(jnp.int32, (rows, columns), 1)
    hit = c == r + offsets[0]
    for offset in offsets[1:]:
        hit = hit | (c == r + offset)
    return jnp.where(hit, 1.0, 0.0)


def mm(a, b, precision=None):
    return jnp.dot(a, b, preferred_element_type=jnp.float32, precision=precision)


def mm_nt(a, b):
    return lax.dot_general(a, b, (((1,), (1,)), ((), ())), preferred_element_type=jnp.float32)


def fused_kernel(
    n,
    m_ref,
    e_ref,
    wr_ref,
    wc_ref,
    w1_ref,
    b1_ref,
    w2_ref,
    b2_ref,
    wm_ref,
    bm_ref,
    wh_ref,
    out_ref,
    pk,
    eb,
    ct,
    rt,
    xb,
    rb,
    pc,
    l1,
    rb2,
    pc2,
    wa,
    wb,
    yb,
    sb,
    gb,
    tb,
    send,
    recv,
    esend,
    erecv,
    msend,
    mrecv,
    lsem,
):
    bf, f32 = jnp.bfloat16, jnp.float32
    rows, cols, ch = m_ref.shape
    hr = rows // 2
    width = cols + SIDE
    per = cols // rows
    R = lax.axis_index("row")
    C = lax.axis_index("col")
    O = 1 - C
    group = lax.axis_index("group")
    mesh_type = pl.DeviceIdType.MESH

    barrier = pltpu.get_barrier_semaphore()
    for k in range(n):
        for col in (C, O):
            if k == 0 and col is C:
                continue
            pl.semaphore_signal(
                barrier, inc=1, device_id=(group, lax.rem(R + k, n), col), device_id_type=mesh_type
            )

    low = one_hot(ch, LANES, (0,)).astype(bf)
    high = one_hot(ch, LANES, (HALF,)).astype(bf)
    both = one_hot(ch, LANES, (0, HALF)).astype(bf)
    own_at = pl.multiple_of(SIDE * C, SIDE)
    tile = m_ref[...]
    packed = mm(tile[:hr].reshape(hr * cols, ch), low) + mm(tile[hr:].reshape(hr * cols, ch), high)
    pk[1, :, pl.ds(own_at, cols), :] = packed.astype(bf).reshape(hr, cols, LANES)
    eb[R] = e_ref[...]

    pl.semaphore_wait(barrier, 2 * n - 1)

    def remote(src, dst, s, r, row, col):
        return pltpu.make_async_remote_copy(
            src_ref=src,
            dst_ref=dst,
            send_sem=s,
            recv_sem=r,
            device_id=(group, row, col),
            device_id_type=mesh_type,
        )

    embs = []
    for k in range(1, n):
        copy = remote(
            eb.at[R], eb.at[R], esend.at[k - 1], erecv.at[k - 1], lax.rem(R + k, n), C
        )
        copy.start()
        embs.append(copy)

    own_src = pk.at[1, :, pl.ds(own_at, cols), :]
    side_src = pk.at[1, :, pl.ds(pl.multiple_of(cols - SIDE - (cols - 2 * SIDE) * C, SIDE), SIDE), :]
    side_at = pl.ds(pl.multiple_of(cols * C, SIDE), SIDE)
    above = jnp.maximum(R - 1, 0)
    below = jnp.minimum(R + 1, n - 1)
    to_below = remote(
        own_src, pk.at[0, :, pl.ds(own_at, cols), :], send.at[0], recv.at[0], below, C
    )
    to_above = remote(
        own_src, pk.at[2, :, pl.ds(own_at, cols), :], send.at[1], recv.at[1], above, C
    )
    to_side = remote(side_src, pk.at[1, :, side_at, :], send.at[2], recv.at[2], R, O)
    side_below = remote(side_src, pk.at[0, :, side_at, :], send.at[3], recv.at[3], below, O)
    side_above = remote(side_src, pk.at[2, :, side_at, :], send.at[4], recv.at[4], above, O)

    @pl.when(R < n - 1)
    def _():
        to_below.start()
        side_below.start()

    @pl.when(R > 0)
    def _():
        to_above.start()
        side_above.start()

    to_side.start()

    def pack_weight(w_ref, dst):
        dst[...] = jnp.zeros_like(dst)
        taps = ((0, 0), (0, 2), (1, 0), (1, 2), (2, 0), (2, 2), (0, 1), (2, 1), (1, 1))
        for at, (a, b) in enumerate(taps):
            dst[at * HALF : at * HALF + ch, :] = mm(w_ref[a, b], both).astype(bf)

    pack_weight(w1_ref, wa)
    pack_weight(w2_ref, wb)
    exact = lax.Precision.HIGHEST
    bias1 = mm(b1_ref[...], both.astype(f32), exact)
    bias2 = mm(b2_ref[...], both.astype(f32), exact)
    gap = jnp.zeros((HALF - ch, wr_ref.shape[1]), bf)
    wr = jnp.concatenate([wr_ref[...], gap, wr_ref[...], gap], axis=0)
    wc = jnp.concatenate([wc_ref[...], gap, wc_ref[...], gap], axis=0)
    eye = one_hot(ch, ch, (0,))
    mix_rows = jnp.concatenate([wm_ref[...], jnp.zeros((LANES - ch, ch), bf)], axis=0)
    mix_t = mm_nt(eye.astype(bf), mix_rows).astype(bf)
    bm = jnp.sum(jnp.where(eye > 0, bm_ref[...], 0.0), axis=1, keepdims=True)
    wh = jnp.sum(jnp.where(eye > 0, wh_ref[...], 0.0), axis=1, keepdims=True)

    for copy in embs:
        copy.wait()
    for k in range(n):
        block = eb[k]
        ct[k * rows : (k + 1) * rows, :] = mm_nt(block, wc)
        rt[k] = mm_nt(block, wr)
    col_terms = ct[pl.ds(pl.multiple_of((n * rows - width) * C, 8), width), :]

    to_side.wait()

    @pl.when(R > 0)
    def _():
        to_below.wait_recv()
        side_below.wait_recv()

    @pl.when(R < n - 1)
    def _():
        to_above.wait_recv()
        side_above.wait_recv()

    lane = lax.broadcasted_iota(jnp.int32, (1, LANES), 1)
    lower = lane < HALF
    col_id = lax.broadcasted_iota(jnp.int32, (width, 1), 0)

    def column_pair(v, d):
        before = jnp.where(col_id < d, 0.0, pltpu.roll(v, d, axis=0))
        after = jnp.where(col_id >= width - d, 0.0, pltpu.roll(v, width - d, axis=0))
        return jnp.where(lower, before, after)

    for b in range(3):
        at = jnp.clip(R + b - 1, 0, n - 1)
        terms = rt[at]
        valid = (R > 0) if b == 0 else (R < n - 1) if b == 2 else None
        for i in range(hr):
            v = pk[b, i].astype(f32)
            turned = pltpu.roll(v, HALF, axis=1)
            for half, x in ((0, jnp.where(lower, v, turned)), (1, jnp.where(lower, turned, v))):
                r = i + half * hr
                x = (x + terms[r : r + 1, :] + col_terms).astype(bf)
                x = x.astype(f32)
                if valid is not None:
                    x = jnp.where(valid, x, 0.0)
                row = b * rows + r
                xb[row] = x.astype(bf)
                x = jnp.maximum(x, 0.0)
                rb[row] = x.astype(bf)
                pc[row] = column_pair(x, FIRST_DILATION).astype(bf)

    def conv(p, r, w, first, count, d, at, size):
        window = pl.ds(at, size)

        def take(ref, shift):
            return ref[first + shift : first + shift + count, window, :].reshape(
                count * size, LANES
            )

        outer = jnp.where(lower, take(r, 0).astype(f32), take(r, 2 * d).astype(f32)).astype(bf)
        left = jnp.concatenate(
            [take(p, 0), take(p, d), take(p, 2 * d), outer, take(r, d)], axis=1
        )
        return mm(left, w[...]).reshape(count, size, LANES)

    d2 = SECOND_DILATION
    ext = rows + 2 * d2
    step = 7 if ext % 7 == 0 else 1
    for t in range(0, ext, step):
        acc = conv(pc, rb, wa, t, step, FIRST_DILATION, 0, width)
        for s in range(step):
            u = t + s
            x = (xb[u + FIRST_DILATION].astype(f32) + acc[s] + bias1).astype(bf).astype(f32)
            if u < d2:
                x = jnp.where(R > 0, x, 0.0)
            elif u >= d2 + rows:
                x = jnp.where(R < n - 1, x, 0.0)
            else:
                l1[u - d2] = x.astype(bf)
            x = jnp.maximum(x, 0.0)
            rb2[u] = x.astype(bf)
            pc2[u] = column_pair(x, d2).astype(bf)

    for t in range(0, rows, hr):
        acc = conv(pc2, rb2, wb, t, hr, d2, own_at, cols)
        for s in range(hr):
            base = l1[t + s, pl.ds(own_at, cols), :].astype(f32)
            yb[t + s] = (base + acc[s] + bias2).astype(bf).astype(f32)

    for i in range(hr):
        pair = jnp.where(lower, yb[i], yb[i + hr])
        for j in range(per):
            sb[j, i] = pair[j * rows : (j + 1) * rows, :].astype(bf)

    mine = lax.rem(R, per)
    quarter = lax.div(R, per)
    for j in range(per):
        peer = per * C + j
        is_self = (peer == R) & (quarter == C)
        copy = remote(sb.at[j], gb.at[mine], msend.at[j], mrecv.at[mine], peer, quarter)
        local = pltpu.make_async_copy(sb.at[j], gb.at[j], lsem)

        @pl.when(jnp.logical_not(is_self))
        def _():
            copy.start()

        @pl.when(is_self)
        def _():
            local.start()

    for j in range(per):
        peer = per * C + j
        is_self = (peer == R) & (quarter == C)
        arrival = remote(sb.at[j], gb.at[j], msend.at[j], mrecv.at[j], peer, quarter)
        local = pltpu.make_async_copy(sb.at[j], gb.at[j], lsem)

        @pl.when(jnp.logical_not(is_self))
        def _():
            arrival.wait_recv()

        @pl.when(is_self)
        def _():
            local.wait()

    pad = tb.shape[0] // cols
    for j in range(per):
        for i in range(hr):
            piece = gb[j, i].astype(f32)
            at = (j * rows + i) * pad
            tb[at : at + rows, :] = piece
            at = (j * rows + i + hr) * pad
            tb[at : at + rows, :] = pltpu.roll(piece, HALF, axis=1)

    for c in range(rows):
        mirror = tb[pl.ds(c, cols, stride=pad), :]
        symmetric = ((yb[c] + mirror) * 0.5).astype(bf)
        mixed = mm_nt(mix_t, symmetric) + bm
        out_ref[c : c + 1, :] = jnp.sum(jnp.maximum(mixed, 0.0) * wh, axis=0, keepdims=True)

    @pl.when(R < n - 1)
    def _():
        to_below.wait_send()
        side_below.wait_send()

    @pl.when(R > 0)
    def _():
        to_above.wait_send()
        side_above.wait_send()

    for j in range(per):
        peer = per * C + j
        is_self = (peer == R) & (quarter == C)
        departure = remote(sb.at[j], gb.at[j], msend.at[j], mrecv.at[j], peer, quarter)

        @pl.when(jnp.logical_not(is_self))
        def _():
            departure.wait_send()


def fused(map_in, embedding, w_row, w_col, w1, b1, w2, b2, w_mix, b_mix, w_head):
    rows, cols, ch = map_in.shape
    n = lax.axis_size("row")
    width, ext, per, hr = cols + SIDE, rows + 2 * SECOND_DILATION, cols // rows, rows // 2
    bf, f32 = jnp.bfloat16, jnp.float32
    dma = pltpu.SemaphoreType.DMA
    return pl.pallas_call(
        functools.partial(fused_kernel, n),
        out_shape=jax.ShapeDtypeStruct((rows, cols), f32),
        in_specs=[pl.BlockSpec(memory_space=pltpu.VMEM)] * 11,
        out_specs=pl.BlockSpec(memory_space=pltpu.VMEM),
        scratch_shapes=[
            pltpu.VMEM((3, hr, width, LANES), bf),
            pltpu.VMEM((n, rows, embedding.shape[1]), bf),
            pltpu.VMEM((n * rows, LANES), f32),
            pltpu.VMEM((n, rows, LANES), f32),
            pltpu.VMEM((3 * rows, width, LANES), bf),
            pltpu.VMEM((3 * rows, width, LANES), bf),
            pltpu.VMEM((3 * rows, width, LANES), bf),
            pltpu.VMEM((rows, width, LANES), bf),
            pltpu.VMEM((ext, width, LANES), bf),
            pltpu.VMEM((ext, width, LANES), bf),
            pltpu.VMEM((10 * HALF, LANES), bf),
            pltpu.VMEM((10 * HALF, LANES), bf),
            pltpu.VMEM((rows, cols, LANES), f32),
            pltpu.VMEM((per, hr, rows, LANES), bf),
            pltpu.VMEM((per, hr, rows, LANES), bf),
            pltpu.VMEM((cols * 16, LANES), f32),
            dma((5,)),
            dma((5,)),
            dma((n - 1,)),
            dma((n - 1,)),
            dma((per,)),
            dma((per,)),
            dma,
        ],
        compiler_params=pltpu.CompilerParams(collective_id=0, has_side_effects=True),
    )(
        map_in,
        embedding,
        w_row.T,
        w_col.T,
        w1,
        b1.reshape(1, ch),
        w2,
        b2.reshape(1, ch),
        w_mix,
        b_mix.reshape(1, ch),
        w_head.reshape(1, ch),
    )


def fits(rows, cols, channels, row_count, col_count):
    scratch = 2 * LANES * (cols + SIDE) * (16 * rows + 6 * SECOND_DILATION)
    halo = FIRST_DILATION + SECOND_DILATION
    return (
        scratch <= FUSED_VMEM
        and rows == halo
        and col_count == 2
        and cols % SIDE == 0
        and channels <= 48
        and cols * col_count == rows * row_count
    )


def on_device(
    map_in,
    embedding,
    w_row,
    w_col,
    first_kernel_weight,
    first_bias,
    second_kernel_weight,
    second_bias,
    w_mix,
    b_mix,
    w_head,
):
    patch_rows, patch_columns, channels = map_in.shape
    row_count = lax.axis_size("row")
    if fits(patch_rows, patch_columns, channels, row_count, lax.axis_size("col")):
        return fused(
            map_in,
            embedding,
            w_row,
            w_col,
            first_kernel_weight,
            first_bias,
            second_kernel_weight,
            second_bias,
            w_mix,
            b_mix,
            w_head,
        )
    row_at = lax.axis_index("row")
    col_at = lax.axis_index("col")
    all_bins = lax.all_gather(embedding, "row", axis=0, tiled=True)
    row_terms = jnp.dot(all_bins, w_row, preferred_element_type=jnp.float32)
    col_terms = jnp.dot(all_bins, w_col, preferred_element_type=jnp.float32)
    own_rows = lax.dynamic_slice_in_dim(row_terms, row_at * patch_rows, patch_rows, 0)
    own_cols = lax.dynamic_slice_in_dim(col_terms, col_at * patch_columns, patch_columns, 0)
    contact_grid = (
        map_in.astype(jnp.float32) + own_rows[:, None, :] + own_cols[None, :, :]
    ).astype(jnp.bfloat16)
    first_padded = padded(contact_grid, (("row", 0), ("col", 1)), FIRST_DILATION)
    first_layer = (
        contact_grid.astype(jnp.float32)
        + dilated_conv(
            jnp.maximum(first_padded, 0),
            first_kernel_weight,
            FIRST_DILATION,
            patch_rows,
            patch_columns,
        )
        + first_bias
    ).astype(jnp.bfloat16)
    second_padded = padded(first_layer, (("row", 0), ("col", 1)), SECOND_DILATION)
    second_layer = (
        first_layer.astype(jnp.float32)
        + dilated_conv(
            jnp.maximum(second_padded, 0),
            second_kernel_weight,
            SECOND_DILATION,
            patch_rows,
            patch_columns,
        )
        + second_bias
    ).astype(jnp.bfloat16)
    half_rows = patch_rows // 2
    blocks_per = row_count // 2
    arranged = second_layer.reshape(2, half_rows, blocks_per, patch_rows, channels)
    arranged = arranged.transpose(0, 2, 1, 3, 4).reshape(
        2 * blocks_per, half_rows, patch_rows, channels
    )
    exchanged = lax.all_to_all(
        lax.all_to_all(arranged, "row", split_axis=0, concat_axis=0, tiled=True),
        "col",
        split_axis=0,
        concat_axis=0,
        tiled=True,
    )
    exchanged = exchanged.reshape(2, blocks_per, half_rows, patch_rows, channels)
    top_half = row_at // blocks_per
    kept_part = lax.dynamic_index_in_dim(exchanged, top_half, 0, keepdims=False)
    sent_part = lax.dynamic_index_in_dim(exchanged, 1 - top_half, 0, keepdims=False)
    came_back = swapped(sent_part, "row", blocks_per.bit_length() - 1)
    stacked = jnp.where(
        top_half == 0, jnp.stack([kept_part, came_back]), jnp.stack([came_back, kept_part])
    )
    mirrored = stacked.transpose(3, 1, 0, 2, 4).reshape(patch_rows, patch_columns, channels)
    symmetric = ((second_layer.astype(jnp.float32) + mirrored.astype(jnp.float32)) * 0.5).astype(
        jnp.bfloat16
    )
    mixture = (
        jnp.einsum("rch,hk->rck", symmetric, w_mix, preferred_element_type=jnp.float32) + b_mix
    )
    mixture = jnp.maximum(mixture, 0.0)
    return jnp.sum(mixture * w_head, axis=-1)


def solution(mesh):
    placed = (
        P(("group", "row"), "col", None),
        P(("group", "row"), None),
        P(),
        P(),
        P(),
        P(),
        P(),
        P(),
        P(),
        P(),
        P(),
    )
    return jax.shard_map(
        on_device, mesh=mesh, in_specs=placed, out_specs=P(("group", "row"), "col"), check_vma=False
    )
```

```python
import functools

import jax
import jax.numpy as jnp
from jax import lax
from jax.experimental import pallas as pl
from jax.experimental.pallas import tpu as pltpu
from jax.sharding import PartitionSpec as P

FIRST_DILATION = 4
SECOND_DILATION = 8


def padded(array, sides, width):
    for axis, dim in sides:
        peers, length = (lax.axis_size(axis), array.shape[dim])
        up = [(i, (i + 1) % peers) for i in range(peers - 1)]
        down = [(j, i) for i, j in up]
        last = lax.slice_in_dim(array, length - width, length, axis=dim)
        leading = lax.slice_in_dim(array, 0, width, axis=dim)
        before = lax.ppermute(last, axis, up)
        after = lax.ppermute(leading, axis, down)
        array = jnp.concatenate([before, array, after], axis=dim)
    return array


def swapped(value, axis, bit):
    mask = 2**bit
    pairs = [(source, source ^ mask) for source in range(lax.axis_size(axis))]
    return lax.ppermute(value, axis, pairs)


def dilated_conv(active, weight, spacing, out_rows, out_cols):
    windows = []
    for tap_row in range(3):
        for tap_col in range(3):
            windows.append(
                active[
                    tap_row * spacing : tap_row * spacing + out_rows,
                    tap_col * spacing : tap_col * spacing + out_cols,
                ]
            )
    stacked = jnp.concatenate(windows, axis=-1)
    flat_weight = weight.reshape(9 * weight.shape[2], weight.shape[3])
    return jnp.einsum("rch,hk->rck", stacked, flat_weight, preferred_element_type=jnp.float32)


LANES = 128
HALF = 64
SIDE = 16
FUSED_VMEM = 8 * 2**20


def one_hot(rows, columns, offsets):
    r = lax.broadcasted_iota(jnp.int32, (rows, columns), 0)
    c = lax.broadcasted_iota(jnp.int32, (rows, columns), 1)
    hit = c == r + offsets[0]
    for offset in offsets[1:]:
        hit = hit | (c == r + offset)
    return jnp.where(hit, 1.0, 0.0)


def mm(a, b, precision=None):
    return jnp.dot(a, b, preferred_element_type=jnp.float32, precision=precision)


def mm_nt(a, b):
    return lax.dot_general(a, b, (((1,), (1,)), ((), ())), preferred_element_type=jnp.float32)


def fused_kernel(
    n,
    m_ref,
    e_ref,
    wr_ref,
    wc_ref,
    w1_ref,
    b1_ref,
    w2_ref,
    b2_ref,
    wm_ref,
    bm_ref,
    wh_ref,
    out_ref,
    pk,
    eb,
    ct,
    rt,
    xb,
    rb,
    pc,
    l1,
    rb2,
    pc2,
    wa,
    wb,
    yb,
    sb,
    gb,
    tb,
    send,
    recv,
    esend,
    erecv,
    msend,
    mrecv,
    lsem,
):
    bf, f32 = jnp.bfloat16, jnp.float32
    rows, cols, ch = m_ref.shape
    hr = rows // 2
    width = cols + SIDE
    per = cols // rows
    R = lax.axis_index("row")
    C = lax.axis_index("col")
    O = 1 - C
    group = lax.axis_index("group")
    mesh_type = pl.DeviceIdType.MESH

    barrier = pltpu.get_barrier_semaphore()
    for k in range(n):
        for col in (C, O):
            if k == 0 and col is C:
                continue
            pl.semaphore_signal(
                barrier, inc=1, device_id=(group, lax.rem(R + k, n), col), device_id_type=mesh_type
            )

    low = one_hot(ch, LANES, (0,)).astype(bf)
    high = one_hot(ch, LANES, (HALF,)).astype(bf)
    both = one_hot(ch, LANES, (0, HALF)).astype(bf)
    own_at = pl.multiple_of(SIDE * C, SIDE)
    tile = m_ref[...]
    packed = mm(tile[:hr].reshape(hr * cols, ch), low) + mm(tile[hr:].reshape(hr * cols, ch), high)
    pk[1, :, pl.ds(own_at, cols), :] = packed.astype(bf).reshape(hr, cols, LANES)
    eb[R] = e_ref[...]

    pl.semaphore_wait(barrier, 2 * n - 1)

    def remote(src, dst, s, r, row, col):
        return pltpu.make_async_remote_copy(
            src_ref=src,
            dst_ref=dst,
            send_sem=s,
            recv_sem=r,
            device_id=(group, row, col),
            device_id_type=mesh_type,
        )

    embs = []
    for k in range(1, n):
        copy = remote(
            eb.at[R], eb.at[R], esend.at[k - 1], erecv.at[k - 1], lax.rem(R + k, n), C
        )
        copy.start()
        embs.append(copy)

    own_src = pk.at[1, :, pl.ds(own_at, cols), :]
    side_src = pk.at[1, :, pl.ds(pl.multiple_of(cols - SIDE - (cols - 2 * SIDE) * C, SIDE), SIDE), :]
    side_at = pl.ds(pl.multiple_of(cols * C, SIDE), SIDE)
    above = jnp.maximum(R - 1, 0)
    below = jnp.minimum(R + 1, n - 1)
    to_below = remote(
        own_src, pk.at[0, :, pl.ds(own_at, cols), :], send.at[0], recv.at[0], below, C
    )
    to_above = remote(
        own_src, pk.at[2, :, pl.ds(own_at, cols), :], send.at[1], recv.at[1], above, C
    )
    to_side = remote(side_src, pk.at[1, :, side_at, :], send.at[2], recv.at[2], R, O)
    side_below = remote(side_src, pk.at[0, :, side_at, :], send.at[3], recv.at[3], below, O)
    side_above = remote(side_src, pk.at[2, :, side_at, :], send.at[4], recv.at[4], above, O)

    @pl.when(R < n - 1)
    def _():
        to_below.start()
        side_below.start()

    @pl.when(R > 0)
    def _():
        to_above.start()
        side_above.start()

    to_side.start()

    def pack_weight(w_ref, dst):
        dst[...] = jnp.zeros_like(dst)
        taps = ((0, 0), (0, 2), (1, 0), (1, 2), (2, 0), (2, 2), (0, 1), (2, 1), (1, 1))
        for at, (a, b) in enumerate(taps):
            dst[at * HALF : at * HALF + ch, :] = mm(w_ref[a, b], both).astype(bf)

    pack_weight(w1_ref, wa)
    pack_weight(w2_ref, wb)
    exact = lax.Precision.HIGHEST
    bias1 = mm(b1_ref[...], both.astype(f32), exact)
    bias2 = mm(b2_ref[...], both.astype(f32), exact)
    gap = jnp.zeros((HALF - ch, wr_ref.shape[1]), bf)
    wr = jnp.concatenate([wr_ref[...], gap, wr_ref[...], gap], axis=0)
    wc = jnp.concatenate([wc_ref[...], gap, wc_ref[...], gap], axis=0)
    eye = one_hot(ch, ch, (0,))
    mix_rows = jnp.concatenate([wm_ref[...], jnp.zeros((LANES - ch, ch), bf)], axis=0)
    mix_t = mm_nt(eye.astype(bf), mix_rows).astype(bf)
    bm = jnp.sum(jnp.where(eye > 0, bm_ref[...], 0.0), axis=1, keepdims=True)
    wh = jnp.sum(jnp.where(eye > 0, wh_ref[...], 0.0), axis=1, keepdims=True)

    for copy in embs:
        copy.wait()
    for k in range(n):
        block = eb[k]
        ct[k * rows : (k + 1) * rows, :] = mm_nt(block, wc)
        rt[k] = mm_nt(block, wr)
    col_terms = ct[pl.ds(pl.multiple_of((n * rows - width) * C, 8), width), :]

    to_side.wait()

    @pl.when(R > 0)
    def _():
        to_below.wait_recv()
        side_below.wait_recv()

    @pl.when(R < n - 1)
    def _():
        to_above.wait_recv()
        side_above.wait_recv()

    lane = lax.broadcasted_iota(jnp.int32, (1, LANES), 1)
    lower = lane < HALF
    col_id = lax.broadcasted_iota(jnp.int32, (width, 1), 0)

    def column_pair(v, d):
        before = jnp.where(col_id < d, 0.0, pltpu.roll(v, d, axis=0))
        after = jnp.where(col_id >= width - d, 0.0, pltpu.roll(v, width - d, axis=0))
        return jnp.where(lower, before, after)

    for b in range(3):
        at = jnp.clip(R + b - 1, 0, n - 1)
        terms = rt[at]
        valid = (R > 0) if b == 0 else (R < n - 1) if b == 2 else None
        for i in range(hr):
            v = pk[b, i].astype(f32)
            turned = pltpu.roll(v, HALF, axis=1)
            for half, x in ((0, jnp.where(lower, v, turned)), (1, jnp.where(lower, turned, v))):
                r = i + half * hr
                x = (x + terms[r : r + 1, :] + col_terms).astype(bf)
                x = x.astype(f32)
                if valid is not None:
                    x = jnp.where(valid, x, 0.0)
                row = b * rows + r
                xb[row] = x.astype(bf)
                x = jnp.maximum(x, 0.0)
                rb[row] = x.astype(bf)
                pc[row] = column_pair(x, FIRST_DILATION).astype(bf)

    def conv(p, r, w, first, count, d, at, size):
        window = pl.ds(at, size)

        def take(ref, shift):
            return ref[first + shift : first + shift + count, window, :].reshape(
                count * size, LANES
            )

        outer = jnp.where(lower, take(r, 0).astype(f32), take(r, 2 * d).astype(f32)).astype(bf)
        left = jnp.concatenate(
            [take(p, 0), take(p, d), take(p, 2 * d), outer, take(r, d)], axis=1
        )
        return mm(left, w[...]).reshape(count, size, LANES)

    d2 = SECOND_DILATION
    ext = rows + 2 * d2
    step = 7 if ext % 7 == 0 else 1
    for t in range(0, ext, step):
        acc = conv(pc, rb, wa, t, step, FIRST_DILATION, 0, width)
        for s in range(step):
            u = t + s
            x = (xb[u + FIRST_DILATION].astype(f32) + acc[s] + bias1).astype(bf).astype(f32)
            if u < d2:
                x = jnp.where(R > 0, x, 0.0)
            elif u >= d2 + rows:
                x = jnp.where(R < n - 1, x, 0.0)
            else:
                l1[u - d2] = x.astype(bf)
            x = jnp.maximum(x, 0.0)
            rb2[u] = x.astype(bf)
            pc2[u] = column_pair(x, d2).astype(bf)

    for t in range(0, rows, hr):
        acc = conv(pc2, rb2, wb, t, hr, d2, own_at, cols)
        for s in range(hr):
            base = l1[t + s, pl.ds(own_at, cols), :].astype(f32)
            yb[t + s] = (base + acc[s] + bias2).astype(bf).astype(f32)

    for i in range(hr):
        pair = jnp.where(lower, yb[i], yb[i + hr])
        for j in range(per):
            sb[j, i] = pair[j * rows : (j + 1) * rows, :].astype(bf)

    mine = lax.rem(R, per)
    quarter = lax.div(R, per)
    for j in range(per):
        peer = per * C + j
        is_self = (peer == R) & (quarter == C)
        copy = remote(sb.at[j], gb.at[mine], msend.at[j], mrecv.at[mine], peer, quarter)
        local = pltpu.make_async_copy(sb.at[j], gb.at[j], lsem)

        @pl.when(jnp.logical_not(is_self))
        def _():
            copy.start()

        @pl.when(is_self)
        def _():
            local.start()

    for j in range(per):
        peer = per * C + j
        is_self = (peer == R) & (quarter == C)
        arrival = remote(sb.at[j], gb.at[j], msend.at[j], mrecv.at[j], peer, quarter)
        local = pltpu.make_async_copy(sb.at[j], gb.at[j], lsem)

        @pl.when(jnp.logical_not(is_self))
        def _():
            arrival.wait_recv()

        @pl.when(is_self)
        def _():
            local.wait()

    pad = tb.shape[0] // cols
    for j in range(per):
        for i in range(hr):
            piece = gb[j, i].astype(f32)
            at = (j * rows + i) * pad
            tb[at : at + rows, :] = piece
            at = (j * rows + i + hr) * pad
            tb[at : at + rows, :] = pltpu.roll(piece, HALF, axis=1)

    for c in range(rows):
        mirror = tb[pl.ds(c, cols, stride=pad), :]
        symmetric = ((yb[c] + mirror) * 0.5).astype(bf)
        mixed = mm_nt(mix_t, symmetric) + bm
        out_ref[c : c + 1, :] = jnp.sum(jnp.maximum(mixed, 0.0) * wh, axis=0, keepdims=True)

    @pl.when(R < n - 1)
    def _():
        to_below.wait_send()
        side_below.wait_send()

    @pl.when(R > 0)
    def _():
        to_above.wait_send()
        side_above.wait_send()

    for j in range(per):
        peer = per * C + j
        is_self = (peer == R) & (quarter == C)
        departure = remote(sb.at[j], gb.at[j], msend.at[j], mrecv.at[j], peer, quarter)

        @pl.when(jnp.logical_not(is_self))
        def _():
            departure.wait_send()


def fused(map_in, embedding, w_row, w_col, w1, b1, w2, b2, w_mix, b_mix, w_head):
    rows, cols, ch = map_in.shape
    n = lax.axis_size("row")
    width, ext, per, hr = cols + SIDE, rows + 2 * SECOND_DILATION, cols // rows, rows // 2
    bf, f32 = jnp.bfloat16, jnp.float32
    dma = pltpu.SemaphoreType.DMA
    return pl.pallas_call(
        functools.partial(fused_kernel, n),
        out_shape=pltpu.VMEM((rows, cols), f32),
        in_specs=[pl.BlockSpec(memory_space=pltpu.VMEM)] * 11,
        out_specs=pl.BlockSpec(memory_space=pltpu.VMEM),
        scratch_shapes=[
            pltpu.VMEM((3, hr, width, LANES), bf),
            pltpu.VMEM((n, rows, embedding.shape[1]), bf),
            pltpu.VMEM((n * rows, LANES), f32),
            pltpu.VMEM((n, rows, LANES), f32),
            pltpu.VMEM((3 * rows, width, LANES), bf),
            pltpu.VMEM((3 * rows, width, LANES), bf),
            pltpu.VMEM((3 * rows, width, LANES), bf),
            pltpu.VMEM((rows, width, LANES), bf),
            pltpu.VMEM((ext, width, LANES), bf),
            pltpu.VMEM((ext, width, LANES), bf),
            pltpu.VMEM((10 * HALF, LANES), bf),
            pltpu.VMEM((10 * HALF, LANES), bf),
            pltpu.VMEM((rows, cols, LANES), f32),
            pltpu.VMEM((per, hr, rows, LANES), bf),
            pltpu.VMEM((per, hr, rows, LANES), bf),
            pltpu.VMEM((cols * 16, LANES), f32),
            dma((5,)),
            dma((5,)),
            dma((n - 1,)),
            dma((n - 1,)),
            dma((per,)),
            dma((per,)),
            dma,
        ],
        compiler_params=pltpu.CompilerParams(collective_id=0, has_side_effects=True),
    )(
        map_in,
        embedding,
        w_row.T,
        w_col.T,
        w1,
        b1.reshape(1, ch),
        w2,
        b2.reshape(1, ch),
        w_mix,
        b_mix.reshape(1, ch),
        w_head.reshape(1, ch),
    )


def fits(rows, cols, channels, row_count, col_count):
    scratch = 2 * LANES * (cols + SIDE) * (16 * rows + 6 * SECOND_DILATION)
    halo = FIRST_DILATION + SECOND_DILATION
    return (
        scratch <= FUSED_VMEM
        and rows == halo
        and col_count == 2
        and cols % SIDE == 0
        and channels <= 48
        and cols * col_count == rows * row_count
    )


def on_device(
    map_in,
    embedding,
    w_row,
    w_col,
    first_kernel_weight,
    first_bias,
    second_kernel_weight,
    second_bias,
    w_mix,
    b_mix,
    w_head,
):
    patch_rows, patch_columns, channels = map_in.shape
    row_count = lax.axis_size("row")
    if fits(patch_rows, patch_columns, channels, row_count, lax.axis_size("col")):
        return fused(
            map_in,
            embedding,
            w_row,
            w_col,
            first_kernel_weight,
            first_bias,
            second_kernel_weight,
            second_bias,
            w_mix,
            b_mix,
            w_head,
        )
    row_at = lax.axis_index("row")
    col_at = lax.axis_index("col")
    all_bins = lax.all_gather(embedding, "row", axis=0, tiled=True)
    row_terms = jnp.dot(all_bins, w_row, preferred_element_type=jnp.float32)
    col_terms = jnp.dot(all_bins, w_col, preferred_element_type=jnp.float32)
    own_rows = lax.dynamic_slice_in_dim(row_terms, row_at * patch_rows, patch_rows, 0)
    own_cols = lax.dynamic_slice_in_dim(col_terms, col_at * patch_columns, patch_columns, 0)
    contact_grid = (
        map_in.astype(jnp.float32) + own_rows[:, None, :] + own_cols[None, :, :]
    ).astype(jnp.bfloat16)
    first_padded = padded(contact_grid, (("row", 0), ("col", 1)), FIRST_DILATION)
    first_layer = (
        contact_grid.astype(jnp.float32)
        + dilated_conv(
            jnp.maximum(first_padded, 0),
            first_kernel_weight,
            FIRST_DILATION,
            patch_rows,
            patch_columns,
        )
        + first_bias
    ).astype(jnp.bfloat16)
    second_padded = padded(first_layer, (("row", 0), ("col", 1)), SECOND_DILATION)
    second_layer = (
        first_layer.astype(jnp.float32)
        + dilated_conv(
            jnp.maximum(second_padded, 0),
            second_kernel_weight,
            SECOND_DILATION,
            patch_rows,
            patch_columns,
        )
        + second_bias
    ).astype(jnp.bfloat16)
    half_rows = patch_rows // 2
    blocks_per = row_count // 2
    arranged = second_layer.reshape(2, half_rows, blocks_per, patch_rows, channels)
    arranged = arranged.transpose(0, 2, 1, 3, 4).reshape(
        2 * blocks_per, half_rows, patch_rows, channels
    )
    exchanged = lax.all_to_all(
        lax.all_to_all(arranged, "row", split_axis=0, concat_axis=0, tiled=True),
        "col",
        split_axis=0,
        concat_axis=0,
        tiled=True,
    )
    exchanged = exchanged.reshape(2, blocks_per, half_rows, patch_rows, channels)
    top_half = row_at // blocks_per
    kept_part = lax.dynamic_index_in_dim(exchanged, top_half, 0, keepdims=False)
    sent_part = lax.dynamic_index_in_dim(exchanged, 1 - top_half, 0, keepdims=False)
    came_back = swapped(sent_part, "row", blocks_per.bit_length() - 1)
    stacked = jnp.where(
        top_half == 0, jnp.stack([kept_part, came_back]), jnp.stack([came_back, kept_part])
    )
    mirrored = stacked.transpose(3, 1, 0, 2, 4).reshape(patch_rows, patch_columns, channels)
    symmetric = ((second_layer.astype(jnp.float32) + mirrored.astype(jnp.float32)) * 0.5).astype(
        jnp.bfloat16
    )
    mixture = (
        jnp.einsum("rch,hk->rck", symmetric, w_mix, preferred_element_type=jnp.float32) + b_mix
    )
    mixture = jnp.maximum(mixture, 0.0)
    return jnp.sum(mixture * w_head, axis=-1)


def solution(mesh):
    placed = (
        P(("group", "row"), "col", None),
        P(("group", "row"), None),
        P(),
        P(),
        P(),
        P(),
        P(),
        P(),
        P(),
        P(),
        P(),
    )
    return jax.shard_map(
        on_device, mesh=mesh, in_specs=placed, out_specs=P(("group", "row"), "col"), check_vma=False
    )
```

```python
import functools

import jax
import jax.numpy as jnp
from jax import lax
from jax.experimental import pallas as pl
from jax.experimental.pallas import tpu as pltpu
from jax.sharding import PartitionSpec as P

FIRST_DILATION = 4
SECOND_DILATION = 8


def padded(array, sides, width):
    for axis, dim in sides:
        peers, length = (lax.axis_size(axis), array.shape[dim])
        up = [(i, (i + 1) % peers) for i in range(peers - 1)]
        down = [(j, i) for i, j in up]
        last = lax.slice_in_dim(array, length - width, length, axis=dim)
        leading = lax.slice_in_dim(array, 0, width, axis=dim)
        before = lax.ppermute(last, axis, up)
        after = lax.ppermute(leading, axis, down)
        array = jnp.concatenate([before, array, after], axis=dim)
    return array


def swapped(value, axis, bit):
    mask = 2**bit
    pairs = [(source, source ^ mask) for source in range(lax.axis_size(axis))]
    return lax.ppermute(value, axis, pairs)


def dilated_conv(active, weight, spacing, out_rows, out_cols):
    windows = []
    for tap_row in range(3):
        for tap_col in range(3):
            windows.append(
                active[
                    tap_row * spacing : tap_row * spacing + out_rows,
                    tap_col * spacing : tap_col * spacing + out_cols,
                ]
            )
    stacked = jnp.concatenate(windows, axis=-1)
    flat_weight = weight.reshape(9 * weight.shape[2], weight.shape[3])
    return jnp.einsum("rch,hk->rck", stacked, flat_weight, preferred_element_type=jnp.float32)


LANES = 128
HALF = 64
SIDE = 16
FUSED_VMEM = 8 * 2**20


def one_hot(rows, columns, offsets):
    r = lax.broadcasted_iota(jnp.int32, (rows, columns), 0)
    c = lax.broadcasted_iota(jnp.int32, (rows, columns), 1)
    hit = c == r + offsets[0]
    for offset in offsets[1:]:
        hit = hit | (c == r + offset)
    return jnp.where(hit, 1.0, 0.0)


def mm(a, b, precision=None):
    return jnp.dot(a, b, preferred_element_type=jnp.float32, precision=precision)


def mm_nt(a, b):
    return lax.dot_general(a, b, (((1,), (1,)), ((), ())), preferred_element_type=jnp.float32)


def fused_kernel(
    n,
    m_hbm,
    e_hbm,
    wr_hbm,
    wc_hbm,
    w1_hbm,
    b1_hbm,
    w2_hbm,
    b2_hbm,
    wm_hbm,
    bm_hbm,
    wh_hbm,
    out_ref,
    pk,
    eb,
    ct,
    rt,
    xb,
    rb,
    pc,
    l1,
    rb2,
    pc2,
    wa,
    wb,
    yb,
    sb,
    gb,
    tb,
    send,
    recv,
    esend,
    erecv,
    msend,
    mrecv,
    lsem,
    isem,
    m_ref,
    e_ref,
    wr_ref,
    wc_ref,
    w1_ref,
    b1_ref,
    w2_ref,
    b2_ref,
    wm_ref,
    bm_ref,
    wh_ref,
):
    bf, f32 = jnp.bfloat16, jnp.float32
    rows, cols, ch = m_ref.shape
    hr = rows // 2
    width = cols + SIDE
    per = cols // rows
    R = lax.axis_index("row")
    C = lax.axis_index("col")
    O = 1 - C
    group = lax.axis_index("group")
    mesh_type = pl.DeviceIdType.MESH

    barrier = pltpu.get_barrier_semaphore()
    for k in range(n):
        for col in (C, O):
            if k == 0 and col is C:
                continue
            pl.semaphore_signal(
                barrier, inc=1, device_id=(group, lax.rem(R + k, n), col), device_id_type=mesh_type
            )

    inputs = (
        (m_hbm, m_ref),
        (e_hbm, e_ref),
        (wr_hbm, wr_ref),
        (wc_hbm, wc_ref),
        (w1_hbm, w1_ref),
        (b1_hbm, b1_ref),
        (w2_hbm, w2_ref),
        (b2_hbm, b2_ref),
        (wm_hbm, wm_ref),
        (bm_hbm, bm_ref),
        (wh_hbm, wh_ref),
    )
    loads = [pltpu.make_async_copy(a, b, isem.at[i]) for i, (a, b) in enumerate(inputs)]
    for load in loads:
        load.start()

    low = one_hot(ch, LANES, (0,)).astype(bf)
    high = one_hot(ch, LANES, (HALF,)).astype(bf)
    both = one_hot(ch, LANES, (0, HALF)).astype(bf)
    own_at = pl.multiple_of(SIDE * C, SIDE)
    loads[0].wait()
    tile = m_ref[...]
    packed = mm(tile[:hr].reshape(hr * cols, ch), low) + mm(tile[hr:].reshape(hr * cols, ch), high)
    pk[1, :, pl.ds(own_at, cols), :] = packed.astype(bf).reshape(hr, cols, LANES)
    loads[1].wait()
    eb[R] = e_ref[...]

    pl.semaphore_wait(barrier, 2 * n - 1)

    def remote(src, dst, s, r, row, col):
        return pltpu.make_async_remote_copy(
            src_ref=src,
            dst_ref=dst,
            send_sem=s,
            recv_sem=r,
            device_id=(group, row, col),
            device_id_type=mesh_type,
        )

    embs = []
    for k in range(1, n):
        copy = remote(
            eb.at[R], eb.at[R], esend.at[k - 1], erecv.at[k - 1], lax.rem(R + k, n), C
        )
        copy.start()
        embs.append(copy)

    own_src = pk.at[1, :, pl.ds(own_at, cols), :]
    side_src = pk.at[1, :, pl.ds(pl.multiple_of(cols - SIDE - (cols - 2 * SIDE) * C, SIDE), SIDE), :]
    side_at = pl.ds(pl.multiple_of(cols * C, SIDE), SIDE)
    above = jnp.maximum(R - 1, 0)
    below = jnp.minimum(R + 1, n - 1)
    to_below = remote(
        own_src, pk.at[0, :, pl.ds(own_at, cols), :], send.at[0], recv.at[0], below, C
    )
    to_above = remote(
        own_src, pk.at[2, :, pl.ds(own_at, cols), :], send.at[1], recv.at[1], above, C
    )
    to_side = remote(side_src, pk.at[1, :, side_at, :], send.at[2], recv.at[2], R, O)
    side_below = remote(side_src, pk.at[0, :, side_at, :], send.at[3], recv.at[3], below, O)
    side_above = remote(side_src, pk.at[2, :, side_at, :], send.at[4], recv.at[4], above, O)

    @pl.when(R < n - 1)
    def _():
        to_below.start()
        side_below.start()

    @pl.when(R > 0)
    def _():
        to_above.start()
        side_above.start()

    to_side.start()

    def pack_weight(w_ref, dst):
        dst[...] = jnp.zeros_like(dst)
        taps = ((0, 0), (0, 2), (1, 0), (1, 2), (2, 0), (2, 2), (0, 1), (2, 1), (1, 1))
        for at, (a, b) in enumerate(taps):
            dst[at * HALF : at * HALF + ch, :] = mm(w_ref[a, b], both).astype(bf)

    for load in loads[2:]:
        load.wait()
    pack_weight(w1_ref, wa)
    pack_weight(w2_ref, wb)
    exact = lax.Precision.HIGHEST
    bias1 = mm(b1_ref[...], both.astype(f32), exact)
    bias2 = mm(b2_ref[...], both.astype(f32), exact)
    gap = jnp.zeros((HALF - ch, wr_ref.shape[1]), bf)
    wr = jnp.concatenate([wr_ref[...], gap, wr_ref[...], gap], axis=0)
    wc = jnp.concatenate([wc_ref[...], gap, wc_ref[...], gap], axis=0)
    eye = one_hot(ch, ch, (0,))
    mix_rows = jnp.concatenate([wm_ref[...], jnp.zeros((LANES - ch, ch), bf)], axis=0)
    mix_t = mm_nt(eye.astype(bf), mix_rows).astype(bf)
    bm = jnp.sum(jnp.where(eye > 0, bm_ref[...], 0.0), axis=1, keepdims=True)
    wh = jnp.sum(jnp.where(eye > 0, wh_ref[...], 0.0), axis=1, keepdims=True)

    for copy in embs:
        copy.wait()
    for k in range(n):
        block = eb[k]
        ct[k * rows : (k + 1) * rows, :] = mm_nt(block, wc)
        rt[k] = mm_nt(block, wr)
    col_terms = ct[pl.ds(pl.multiple_of((n * rows - width) * C, 8), width), :]

    to_side.wait()

    @pl.when(R > 0)
    def _():
        to_below.wait_recv()
        side_below.wait_recv()

    @pl.when(R < n - 1)
    def _():
        to_above.wait_recv()
        side_above.wait_recv()

    lane = lax.broadcasted_iota(jnp.int32, (1, LANES), 1)
    lower = lane < HALF
    col_id = lax.broadcasted_iota(jnp.int32, (width, 1), 0)

    def column_pair(v, d):
        before = jnp.where(col_id < d, 0.0, pltpu.roll(v, d, axis=0))
        after = jnp.where(col_id >= width - d, 0.0, pltpu.roll(v, width - d, axis=0))
        return jnp.where(lower, before, after)

    for b in range(3):
        at = jnp.clip(R + b - 1, 0, n - 1)
        terms = rt[at]
        valid = (R > 0) if b == 0 else (R < n - 1) if b == 2 else None
        for i in range(hr):
            v = pk[b, i].astype(f32)
            turned = pltpu.roll(v, HALF, axis=1)
            for half, x in ((0, jnp.where(lower, v, turned)), (1, jnp.where(lower, turned, v))):
                r = i + half * hr
                x = (x + terms[r : r + 1, :] + col_terms).astype(bf)
                x = x.astype(f32)
                if valid is not None:
                    x = jnp.where(valid, x, 0.0)
                row = b * rows + r
                xb[row] = x.astype(bf)
                x = jnp.maximum(x, 0.0)
                rb[row] = x.astype(bf)
                pc[row] = column_pair(x, FIRST_DILATION).astype(bf)

    def conv(p, r, w, first, count, d, at, size):
        window = pl.ds(at, size)

        def take(ref, shift):
            return ref[first + shift : first + shift + count, window, :].reshape(
                count * size, LANES
            )

        outer = jnp.where(lower, take(r, 0).astype(f32), take(r, 2 * d).astype(f32)).astype(bf)
        left = jnp.concatenate(
            [take(p, 0), take(p, d), take(p, 2 * d), outer, take(r, d)], axis=1
        )
        return mm(left, w[...]).reshape(count, size, LANES)

    d2 = SECOND_DILATION
    ext = rows + 2 * d2
    step = 7 if ext % 7 == 0 else 1
    for t in range(0, ext, step):
        acc = conv(pc, rb, wa, t, step, FIRST_DILATION, 0, width)
        for s in range(step):
            u = t + s
            x = (xb[u + FIRST_DILATION].astype(f32) + acc[s] + bias1).astype(bf).astype(f32)
            if u < d2:
                x = jnp.where(R > 0, x, 0.0)
            elif u >= d2 + rows:
                x = jnp.where(R < n - 1, x, 0.0)
            else:
                l1[u - d2] = x.astype(bf)
            x = jnp.maximum(x, 0.0)
            rb2[u] = x.astype(bf)
            pc2[u] = column_pair(x, d2).astype(bf)

    for t in range(0, rows, hr):
        acc = conv(pc2, rb2, wb, t, hr, d2, own_at, cols)
        for s in range(hr):
            base = l1[t + s, pl.ds(own_at, cols), :].astype(f32)
            yb[t + s] = (base + acc[s] + bias2).astype(bf).astype(f32)

    for i in range(hr):
        pair = jnp.where(lower, yb[i], yb[i + hr])
        for j in range(per):
            sb[j, i] = pair[j * rows : (j + 1) * rows, :].astype(bf)

    mine = lax.rem(R, per)
    quarter = lax.div(R, per)
    for j in range(per):
        peer = per * C + j
        is_self = (peer == R) & (quarter == C)
        copy = remote(sb.at[j], gb.at[mine], msend.at[j], mrecv.at[mine], peer, quarter)
        local = pltpu.make_async_copy(sb.at[j], gb.at[j], lsem)

        @pl.when(jnp.logical_not(is_self))
        def _():
            copy.start()

        @pl.when(is_self)
        def _():
            local.start()

    for j in range(per):
        peer = per * C + j
        is_self = (peer == R) & (quarter == C)
        arrival = remote(sb.at[j], gb.at[j], msend.at[j], mrecv.at[j], peer, quarter)
        local = pltpu.make_async_copy(sb.at[j], gb.at[j], lsem)

        @pl.when(jnp.logical_not(is_self))
        def _():
            arrival.wait_recv()

        @pl.when(is_self)
        def _():
            local.wait()

    pad = tb.shape[0] // cols
    for j in range(per):
        for i in range(hr):
            piece = gb[j, i].astype(f32)
            at = (j * rows + i) * pad
            tb[at : at + rows, :] = piece
            at = (j * rows + i + hr) * pad
            tb[at : at + rows, :] = pltpu.roll(piece, HALF, axis=1)

    for c in range(rows):
        mirror = tb[pl.ds(c, cols, stride=pad), :]
        symmetric = ((yb[c] + mirror) * 0.5).astype(bf)
        mixed = mm_nt(mix_t, symmetric) + bm
        out_ref[c : c + 1, :] = jnp.sum(jnp.maximum(mixed, 0.0) * wh, axis=0, keepdims=True)

    @pl.when(R < n - 1)
    def _():
        to_below.wait_send()
        side_below.wait_send()

    @pl.when(R > 0)
    def _():
        to_above.wait_send()
        side_above.wait_send()

    for j in range(per):
        peer = per * C + j
        is_self = (peer == R) & (quarter == C)
        departure = remote(sb.at[j], gb.at[j], msend.at[j], mrecv.at[j], peer, quarter)

        @pl.when(jnp.logical_not(is_self))
        def _():
            departure.wait_send()


def fused(map_in, embedding, w_row, w_col, w1, b1, w2, b2, w_mix, b_mix, w_head):
    rows, cols, ch = map_in.shape
    n = lax.axis_size("row")
    width, ext, per, hr = cols + SIDE, rows + 2 * SECOND_DILATION, cols // rows, rows // 2
    bf, f32 = jnp.bfloat16, jnp.float32
    dma = pltpu.SemaphoreType.DMA
    operands = (
        map_in,
        embedding,
        w_row.T,
        w_col.T,
        w1,
        b1.reshape(1, ch),
        w2,
        b2.reshape(1, ch),
        w_mix,
        b_mix.reshape(1, ch),
        w_head.reshape(1, ch),
    )
    return pl.pallas_call(
        functools.partial(fused_kernel, n),
        out_shape=pltpu.VMEM((rows, cols), f32),
        in_specs=[pl.BlockSpec(memory_space=pl.ANY)] * 11,
        out_specs=pl.BlockSpec(memory_space=pltpu.VMEM),
        scratch_shapes=[
            pltpu.VMEM((3, hr, width, LANES), bf),
            pltpu.VMEM((n, rows, embedding.shape[1]), bf),
            pltpu.VMEM((n * rows, LANES), f32),
            pltpu.VMEM((n, rows, LANES), f32),
            pltpu.VMEM((3 * rows, width, LANES), bf),
            pltpu.VMEM((3 * rows, width, LANES), bf),
            pltpu.VMEM((3 * rows, width, LANES), bf),
            pltpu.VMEM((rows, width, LANES), bf),
            pltpu.VMEM((ext, width, LANES), bf),
            pltpu.VMEM((ext, width, LANES), bf),
            pltpu.VMEM((10 * HALF, LANES), bf),
            pltpu.VMEM((10 * HALF, LANES), bf),
            pltpu.VMEM((rows, cols, LANES), f32),
            pltpu.VMEM((per, hr, rows, LANES), bf),
            pltpu.VMEM((per, hr, rows, LANES), bf),
            pltpu.VMEM((cols * 16, LANES), f32),
            dma((5,)),
            dma((5,)),
            dma((n - 1,)),
            dma((n - 1,)),
            dma((per,)),
            dma((per,)),
            dma,
            dma((11,)),
            *[pltpu.VMEM(x.shape, x.dtype) for x in operands],
        ],
        compiler_params=pltpu.CompilerParams(collective_id=0, has_side_effects=True),
    )(*operands)


def fits(rows, cols, channels, row_count, col_count):
    scratch = 2 * LANES * (cols + SIDE) * (16 * rows + 6 * SECOND_DILATION)
    halo = FIRST_DILATION + SECOND_DILATION
    return (
        scratch <= FUSED_VMEM
        and rows == halo
        and col_count == 2
        and cols % SIDE == 0
        and channels <= 48
        and cols * col_count == rows * row_count
    )


def on_device(
    map_in,
    embedding,
    w_row,
    w_col,
    first_kernel_weight,
    first_bias,
    second_kernel_weight,
    second_bias,
    w_mix,
    b_mix,
    w_head,
):
    patch_rows, patch_columns, channels = map_in.shape
    row_count = lax.axis_size("row")
    if fits(patch_rows, patch_columns, channels, row_count, lax.axis_size("col")):
        return fused(
            map_in,
            embedding,
            w_row,
            w_col,
            first_kernel_weight,
            first_bias,
            second_kernel_weight,
            second_bias,
            w_mix,
            b_mix,
            w_head,
        )
    row_at = lax.axis_index("row")
    col_at = lax.axis_index("col")
    all_bins = lax.all_gather(embedding, "row", axis=0, tiled=True)
    row_terms = jnp.dot(all_bins, w_row, preferred_element_type=jnp.float32)
    col_terms = jnp.dot(all_bins, w_col, preferred_element_type=jnp.float32)
    own_rows = lax.dynamic_slice_in_dim(row_terms, row_at * patch_rows, patch_rows, 0)
    own_cols = lax.dynamic_slice_in_dim(col_terms, col_at * patch_columns, patch_columns, 0)
    contact_grid = (
        map_in.astype(jnp.float32) + own_rows[:, None, :] + own_cols[None, :, :]
    ).astype(jnp.bfloat16)
    first_padded = padded(contact_grid, (("row", 0), ("col", 1)), FIRST_DILATION)
    first_layer = (
        contact_grid.astype(jnp.float32)
        + dilated_conv(
            jnp.maximum(first_padded, 0),
            first_kernel_weight,
            FIRST_DILATION,
            patch_rows,
            patch_columns,
        )
        + first_bias
    ).astype(jnp.bfloat16)
    second_padded = padded(first_layer, (("row", 0), ("col", 1)), SECOND_DILATION)
    second_layer = (
        first_layer.astype(jnp.float32)
        + dilated_conv(
            jnp.maximum(second_padded, 0),
            second_kernel_weight,
            SECOND_DILATION,
            patch_rows,
            patch_columns,
        )
        + second_bias
    ).astype(jnp.bfloat16)
    half_rows = patch_rows // 2
    blocks_per = row_count // 2
    arranged = second_layer.reshape(2, half_rows, blocks_per, patch_rows, channels)
    arranged = arranged.transpose(0, 2, 1, 3, 4).reshape(
        2 * blocks_per, half_rows, patch_rows, channels
    )
    exchanged = lax.all_to_all(
        lax.all_to_all(arranged, "row", split_axis=0, concat_axis=0, tiled=True),
        "col",
        split_axis=0,
        concat_axis=0,
        tiled=True,
    )
    exchanged = exchanged.reshape(2, blocks_per, half_rows, patch_rows, channels)
    top_half = row_at // blocks_per
    kept_part = lax.dynamic_index_in_dim(exchanged, top_half, 0, keepdims=False)
    sent_part = lax.dynamic_index_in_dim(exchanged, 1 - top_half, 0, keepdims=False)
    came_back = swapped(sent_part, "row", blocks_per.bit_length() - 1)
    stacked = jnp.where(
        top_half == 0, jnp.stack([kept_part, came_back]), jnp.stack([came_back, kept_part])
    )
    mirrored = stacked.transpose(3, 1, 0, 2, 4).reshape(patch_rows, patch_columns, channels)
    symmetric = ((second_layer.astype(jnp.float32) + mirrored.astype(jnp.float32)) * 0.5).astype(
        jnp.bfloat16
    )
    mixture = (
        jnp.einsum("rch,hk->rck", symmetric, w_mix, preferred_element_type=jnp.float32) + b_mix
    )
    mixture = jnp.maximum(mixture, 0.0)
    return jnp.sum(mixture * w_head, axis=-1)


def solution(mesh):
    placed = (
        P(("group", "row"), "col", None),
        P(("group", "row"), None),
        P(),
        P(),
        P(),
        P(),
        P(),
        P(),
        P(),
        P(),
        P(),
    )
    return jax.shard_map(
        on_device, mesh=mesh, in_specs=placed, out_specs=P(("group", "row"), "col"), check_vma=False
    )
```
